128 devices in a mesh: seq: 32 (over y, x, z_lo), tp: 4 (over z_hi, core).
Axes of the slice: x: 4, y: 4, z: 4 (z_hi: 2, z_lo: 2; z = z_hi * 2 + z_lo), core: 2. Of those that a mesh axis runs over, the one named last changes fastest.
Arguments:
- hidden_in: bfloat16 [24576, 4096], P(('seq', 'tp')), may hold values from -26 to 26
- norm_gain: float32 [4096], replicated, may hold values from 0.1 to 1.9
- w_qkv: bfloat16 [3, 4096, 2048], P(None, None, 'tp'), may hold values from -1 to 1
- w_out: bfloat16 [2048, 4096], P('tp'), may hold values from -0.125 to 0.125
Outputs:
- datastore: bfloat16 [24576, 4096], P(('seq', 'tp'))
The draws below stay inside these ranges and needn't reach their ends.
All inputs are finite; a program needn't handle non-finite values.
Results may differ from the reference program's by a relative error of at most 0.006.
Values may be sent and summed in bfloat16 or wider, within the bound.
A program may use at most 128 MiB of HBM per device.

```python
import math
import jax
import jax.numpy as jnp
from jax import lax

D = 4096
HEADS = 32
HD = 64
SPAN = 512
TOKENS = 24576
STRIPE = 6
N_SEQ = 32
N_TP = 4


def draw_hidden_in(key, part):
    key_one = jax.random.fold_in(jax.random.fold_in(key, 11), 0)
    result = jnp.clip(jax.random.normal(key_one, (TOKENS, D), jnp.float32), -6.0, 6.0)
    return result.astype(jnp.bfloat16)


def draw_w_qkv(key, part):
    key_one = jax.random.fold_in(jax.random.fold_in(key, 23), 0)
    scaling = jnp.array([0.3, 1.0, 1.0], jnp.float32)[:, None, None] / math.sqrt(D)
    result = jnp.clip(jax.random.normal(key_one, (3, D, HEADS * HD), jnp.float32), -6.0, 6.0) * scaling
    return result.astype(jnp.bfloat16)


def block_scale(key, extent, cuts, least, high):
    gain, own = 1.0, jax.random.fold_in(key, 6)
    for dim, shards_of in cuts:
        draws = jnp.exp(jax.random.uniform(jax.random.fold_in(own, dim), (shards_of,), jnp.float32, least / len(cuts), high / len(cuts)))
        gain = gain * jnp.repeat(draws, extent[dim] // shards_of).reshape([-1 if axis == dim else 1 for axis in range(len(extent))])
    return gain


def centred(rng, shape, width, most, shards=(), held_as=jnp.bfloat16):
    gain = block_scale(rng, shape, shards, -0.22, 0.18) if shards else 1.0
    values = jax.random.normal(rng, shape, jnp.float32) * width * gain
    return jnp.minimum(jnp.maximum(values, -most), most).astype(held_as)


def setup_inputs(seed: int = 0) -> dict:
    seeds = jax.random.split(jax.random.key(seed), 5)
    hidden_in = draw_hidden_in(jax.random.fold_in(seeds[4], 71), 0)
    norm_gain = jnp.clip(1.0 + 0.18 * jax.random.normal(seeds[1], (D,), jnp.float32), 0.1, 1.9)
    w_qkv = draw_w_qkv(jax.random.fold_in(seeds[4], 71), 0)
    w_out = centred(seeds[3], (HEADS * HD, D), (HEADS * HD) ** -0.5, 0.125, ((0, 4),))
    return {"hidden_in": hidden_in, "norm_gain": norm_gain, "w_qkv": w_qkv, "w_out": w_out}


epsilon = 1e-06

def reference(hidden_in, norm_gain, w_qkv, w_out):
    widened = hidden_in.astype(jnp.float32)
    mean_square = lax.optimization_barrier(jnp.mean(widened * widened, axis=1, keepdims=True))
    normed = (widened * lax.rsqrt(mean_square + epsilon) * norm_gain[None, :]).astype(jnp.bfloat16)
    queries = jnp.dot(normed, w_qkv[0], preferred_element_type=jnp.float32).astype(jnp.bfloat16)
    keys_all = jnp.dot(normed, w_qkv[1], preferred_element_type=jnp.float32).astype(jnp.bfloat16)
    values_all = jnp.dot(normed, w_qkv[2], preferred_element_type=jnp.float32).astype(jnp.bfloat16)
    half_len = SPAN // 2
    quarter = SPAN // 4
    pad_keys = jnp.pad(keys_all, ((quarter, quarter), (0, 0)))
    pad_values = jnp.pad(values_all, ((quarter, quarter), (0, 0)))
    block_count = TOKENS // half_len

    def one_block(number):
        start = (number * half_len).astype(jnp.int32)
        query_block = lax.dynamic_slice_in_dim(queries, start, half_len, 0).astype(jnp.float32).reshape(half_len, HEADS, HD)
        key_block = lax.dynamic_slice_in_dim(pad_keys, start, SPAN, 0).astype(jnp.float32).reshape(SPAN, HEADS, HD)
        value_block = lax.dynamic_slice_in_dim(pad_values, start, SPAN, 0).astype(jnp.float32).reshape(SPAN, HEADS, HD)
        scores = jnp.einsum('qhd,khd->hqk', query_block, key_block, precision=lax.Precision.HIGHEST)
        key_place = start - quarter + jnp.arange(SPAN, dtype=jnp.int32)
        key_valid = jnp.logical_and(key_place >= 0, key_place < TOKENS)
        scores = jnp.where(key_valid[None, None, :], scores, -1e+30)
        row_max = lax.optimization_barrier(jnp.max(scores, axis=-1, keepdims=True))
        powers = jnp.exp(scores - row_max)
        weights = (powers / lax.optimization_barrier(jnp.sum(powers, axis=-1, keepdims=True))).astype(jnp.bfloat16)
        context = jnp.einsum('hqk,khd->qhd', weights.astype(jnp.float32), value_block, precision=lax.Precision.HIGHEST)
        return context.astype(jnp.bfloat16).reshape(half_len, HEADS * HD)
    contexts = lax.map(one_block, jnp.arange(block_count, dtype=jnp.int32))
    context = contexts.reshape(TOKENS, HEADS * HD)
    new_state = (widened + jnp.dot(context, w_out, preferred_element_type=jnp.float32)).astype(jnp.bfloat16)
    grouped = new_state.reshape(N_SEQ, N_TP, N_SEQ, STRIPE, D)
    return jnp.transpose(grouped, (2, 1, 0, 3, 4)).reshape(TOKENS, D)
```

```python
import jax
import jax.numpy as jnp
from jax import lax
from jax.experimental import pallas as pl
from jax.experimental.pallas import tpu as pltpu
from jax.sharding import PartitionSpec as P

D = 4096
HD = 64
OWN = 192
HALF = 384
QUARTER = 128
WIDTH = 512
epsilon = 1e-06
MESH = pl.DeviceIdType.MESH
f32 = jnp.float32
bf16 = jnp.bfloat16


def rows(start, size, unit=8):
    return pl.ds(pl.multiple_of(start, unit), size)


def waiter(ref, sem):
    pltpu.make_async_copy(ref, ref, sem).wait()


def spread_matrix():
    i = lax.broadcasted_iota(jnp.int32, (256, OWN), 0)
    j = lax.broadcasted_iota(jnp.int32, (256, OWN), 1)
    r = i & 7
    return jnp.where((r < 6) & (j == (i >> 3) * 6 + r), 1.0, 0.0).astype(bf16)


def gather_matrix():
    i = lax.broadcasted_iota(jnp.int32, (OWN, 256), 1)
    j = lax.broadcasted_iota(jnp.int32, (OWN, 256), 0)
    r = i & 7
    return jnp.where((r < 6) & (j == (i >> 3) * 6 + r), 1.0, 0.0).astype(bf16)


def kernel(
    hid, gain, wqkv, wout, out,
    H, NB, WQ, WO, QKV, CTX, CS, CR, XS, XR, CD,
    loc, wsem, agS, agR, fwS, fwR, sibS, sibR, wsS, wsR, p1S, p1R, s1S, s1R, s2S, s2R, wfS, wfR, hS, hR, kvS, kvR, cS, cR,
):
    s = lax.axis_index("seq")
    t = lax.axis_index("tp")
    y, x, zl = s // 8, lax.rem(s // 2, 4), lax.rem(s, 2)
    zh, c = t // 2, lax.rem(t, 2)
    zo, sib = 1 - zh, 1 - c
    tsib, topp = zh * 2 + sib, zo * 2 + c
    me = s * 4 + t

    barrier = pltpu.get_barrier_semaphore()

    def greet(i, carry):
        o = lax.rem(me + i, 128)
        pl.semaphore_signal(barrier, 1, device_id=(o // 4, lax.rem(o, 4)), device_id_type=MESH)
        return carry

    own_rows = rows(t * OWN, OWN, 64)
    load_h = pltpu.make_async_copy(hid, H.at[own_rows], loc.at[0])
    load_h.start()
    load_wq = pltpu.make_async_copy(wqkv, WQ, loc.at[1])
    load_wq.start()
    load_wo = pltpu.make_async_copy(wout, WO.at[t], loc.at[2])
    load_wo.start()

    lax.fori_loop(1, 128, greet, 0)
    pl.semaphore_wait(barrier, 127)

    def remote(src, dst, ss, rs, seq, tp):
        return pltpu.make_async_remote_copy(src, dst, ss, rs, device_id=(seq, tp), device_id_type=MESH)

    p0, p1 = y * 4 + x, x * 4 + y
    pmine = jnp.where(c == 0, p0, p1)
    seq_cross = y * 8 + x * 2 + (1 - zl)
    first = []
    for cc in range(2):
        cols = pl.ds(cc * 2048, 2048)
        cp = remote(wout.at[rows(pmine * 32, 32, 32), cols], WO.at[t, rows(pmine * 32, 32, 32), cols],
                    p1S.at[cc], p1R.at[c], seq_cross, zo * 2 + cc)
        cp.start()
        first.append(cp)
    to_sib = remote(hid, H.at[own_rows], sibS, sibR, s, tsib)
    to_sib.start()
    ag = []
    for j in range(3):
        cp = remote(hid.at[pl.ds(j * 64, 64)], H.at[rows(t * OWN + j * 64, 64, 64)], agS.at[j], agR.at[j], s, topp)
        cp.start()
        ag.append(cp)
    w_sib = remote(wout, WO.at[t], wsS, wsR, s, tsib)
    w_sib.start()

    load_h.wait()
    spread = spread_matrix()

    def spread_hidden(n, carry):
        cols = rows(n * 512, 512, 512)
        XS[:, cols] = jnp.dot(spread, H[own_rows, cols], preferred_element_type=f32).astype(bf16)
        return carry

    lax.fori_loop(0, 8, spread_hidden, 0)

    def send_hidden(i, carry):
        o = lax.rem(s + i * 11, 32)
        remote(XS.at[rows(o * 8, 8)], XR.at[rows(s * 8, 8)], hS, hR, o, t).start()
        return carry

    lax.fori_loop(1, 32, send_hidden, 0)
    own_hidden = pltpu.make_async_copy(XS.at[rows(s * 8, 8)], XR.at[rows(s * 8, 8)], loc.at[3])
    own_hidden.start()

    def norm(base):
        def body(i, carry):
            w = H[rows(base + i * 16, 16, 16), :].astype(f32)
            scale = lax.rsqrt(jnp.sum(w * w, axis=1, keepdims=True) * (1.0 / D) + epsilon)
            NB[rows(i * 16, 16, 16), :] = (w * scale * gain[...]).astype(bf16)
            return carry
        lax.fori_loop(0, HALF // 16, body, 0)

    def project(base):
        def body(k, carry):
            QKV[k, rows(QUARTER + base, HALF, 128), :] = jnp.dot(
                NB[...], WQ[k], preferred_element_type=f32).astype(bf16)
            return carry
        lax.fori_loop(0, 3, body, 0)

    sh0, sh1 = zo * 2, zo * 2 + 1
    mycols = rows(c * 2048, 2048, 2048)

    waiter(H.at[own_rows], sibR)
    norm(zh * HALF)
    for cc in range(2):
        waiter(WO.at[0, pl.ds(0, 32), pl.ds(0, 2048)], p1R.at[cc])
    second = []
    for d in range(1, 4):
        xo, yo = lax.rem(x + d, 4), lax.rem(y + d, 4)
        sl = WO.at[sh0, rows(p0 * 32, 32, 32), mycols]
        cp = remote(sl, sl, s1S.at[0], s1R.at[0], y * 8 + xo * 2 + zl, t)
        cp.start()
        sl = WO.at[sh1, rows(p1 * 32, 32, 32), mycols]
        cp = remote(sl, sl, s1S.at[1], s1R.at[1], yo * 8 + x * 2 + zl, t)
        cp.start()
    load_wq.wait()
    project(zh * HALF)
    for k in range(2):
        waiter(WO.at[0, pl.ds(0, 96), pl.ds(0, 2048)], s1R.at[k])
    for d in range(1, 4):
        xo, yo = lax.rem(x + d, 4), lax.rem(y + d, 4)
        sl = WO.at[sh0, rows(y * 128, 128, 128), mycols]
        remote(sl, sl, s2S.at[0], s2R.at[0], yo * 8 + x * 2 + zl, t).start()
        sl = WO.at[sh1, rows(x * 128, 128, 128), mycols]
        remote(sl, sl, s2S.at[1], s2R.at[1], y * 8 + xo * 2 + zl, t).start()

    fw = []
    for j in range(3):
        sl = H.at[rows(topp * OWN + j * 64, 64, 64)]
        waiter(sl, agR.at[j])
        cp = remote(sl, sl, fwS.at[j], fwR.at[j], s, tsib)
        cp.start()
        fw.append(cp)
    for j in range(3):
        waiter(H.at[pl.ds(0, 64)], fwR.at[j])
    norm(zo * HALF)
    project(zo * HALF)

    lo = QKV.at[pl.ds(1, 2), pl.ds(0, 128)]
    hi = QKV.at[pl.ds(1, 2), pl.ds(896, 128)]

    @pl.when(s > 0)
    def _():
        remote(QKV.at[pl.ds(1, 2), pl.ds(128, 128)], hi, kvS.at[0], kvR.at[0], s - 1, t).start()

    @pl.when(s < 31)
    def _():
        remote(QKV.at[pl.ds(1, 2), pl.ds(768, 128)], lo, kvS.at[1], kvR.at[1], s + 1, t).start()

    @pl.when(s == 0)
    def _():
        QKV[pl.ds(1, 2), pl.ds(0, 128), :] = jnp.zeros((2, 128, WIDTH), bf16)

    @pl.when(s == 31)
    def _():
        QKV[pl.ds(1, 2), pl.ds(896, 128), :] = jnp.zeros((2, 128, WIDTH), bf16)

    @pl.when(s > 0)
    def _():
        waiter(lo, kvR.at[1])

    @pl.when(s < 31)
    def _():
        waiter(hi, kvR.at[0])

    lane = lax.broadcasted_iota(jnp.int32, (256, 128), 1)
    place = lax.broadcasted_iota(jnp.int32, (1, 512), 1)

    def attend(i, carry):
        b, pair = i // 4, lax.rem(i, 4)
        cols = rows(pair * 128, 128, 128)
        q = QKV[0, rows(QUARTER + b * 256, 256, 128), cols]
        k = QKV[1, rows(b * 256, 512, 128), cols]
        v = QKV[2, rows(b * 256, 512, 128), cols]
        first_ok = jnp.where((s == 0) & (b == 0), 128, 0)
        last_ok = jnp.where((s == 31) & (b == 2), 384, 512)
        bias = jnp.where((place >= first_ok) & (place < last_ok), 0.0, -1e30)
        parts = []
        for h in range(2):
            qh = jnp.where((lane < HD) == (h == 0), q, jnp.zeros_like(q))
            sc = lax.dot_general(qh, k, (((1,), (1,)), ((), ())), preferred_element_type=f32) + bias
            m = jnp.max(sc, axis=1, keepdims=True)
            p = jnp.exp(sc - m)
            total = jnp.sum(p, axis=1, keepdims=True)
            o = jnp.dot(p.astype(bf16), v, preferred_element_type=f32)
            parts.append(o / total)
        CTX[rows(b * 256, 256, 256), cols] = jnp.where(lane < HD, parts[0], parts[1]).astype(bf16)
        return carry

    lax.fori_loop(0, 12, attend, 0)

    def spread_context(n, carry):
        CS[rows(n * 256, 256, 256), :] = jnp.dot(
            spread, CTX[rows(n * OWN, OWN, 64), :], preferred_element_type=f32).astype(bf16)
        return carry

    lax.fori_loop(0, 4, spread_context, 0)
    ccols = rows(t * WIDTH, WIDTH, 512)

    def send_context(i, carry):
        o = lax.rem(me + i * 37, 128)
        os_, ot = o // 4, lax.rem(o, 4)
        remote(CS.at[rows(ot * 256 + os_ * 8, 8)], CR.at[rows(s * 8, 8), ccols], cS, cR, os_, ot).start()
        return carry

    lax.fori_loop(1, 128, send_context, 0)
    own_context = pltpu.make_async_copy(CS.at[rows(t * 256 + s * 8, 8)], CR.at[rows(s * 8, 8), ccols], loc.at[4])
    own_context.start()

    for k in range(2):
        waiter(WO.at[0, pl.ds(0, 384), pl.ds(0, 2048)], s2R.at[k])
    sl = WO.at[pl.ds(zo * 2, 2), :, mycols]
    w_fw = remote(sl, sl, wfS, wfR, s, tsib)
    w_fw.start()

    pack = gather_matrix()
    load_wo.wait()
    waiter(WO.at[0], wsR)
    waiter(WO.at[pl.ds(0, 2), :, pl.ds(0, 2048)], wfR)
    own_hidden.wait()
    waiter(XR.at[pl.ds(0, 248)], hR)
    own_context.wait()
    waiter(CS.at[pl.ds(0, 1016)], cR)
    CD[...] = jnp.dot(pack, CR[...], preferred_element_type=f32).astype(bf16)

    def finish(n, carry):
        cols = rows(n * 512, 512, 512)
        acc = jnp.dot(pack, XR[:, cols], preferred_element_type=f32)
        prod = jnp.zeros((OWN, 512), f32)
        for k in range(4):
            prod += jnp.dot(CD[:, k * 512:(k + 1) * 512], WO[k, :, cols], preferred_element_type=f32)
        out[:, cols] = (acc + prod).astype(bf16)
        return carry

    lax.fori_loop(0, 8, finish, 0)

    for cp in first:
        cp.wait_send()
    to_sib.wait_send()
    for cp in ag + fw:
        cp.wait_send()
    w_sib.wait_send()
    w_fw.wait_send()
    for k in range(2):
        waiter(WO.at[0, pl.ds(0, 96), pl.ds(0, 2048)], s1S.at[k])
        waiter(WO.at[0, pl.ds(0, 384), pl.ds(0, 2048)], s2S.at[k])
    waiter(XS.at[pl.ds(0, 248)], hS)
    waiter(CS.at[pl.ds(0, 1016)], cS)

    @pl.when(s > 0)
    def _():
        waiter(lo, kvS.at[0])

    @pl.when(s < 31)
    def _():
        waiter(hi, kvS.at[1])


def on_device(hidden_in, norm_gain, w_qkv, w_out):
    dma = pltpu.SemaphoreType.DMA
    return pl.pallas_call(
        kernel,
        out_shape=jax.ShapeDtypeStruct((OWN, D), bf16),
        in_specs=[
            pl.BlockSpec(memory_space=pl.ANY),
            pl.BlockSpec(memory_space=pltpu.VMEM),
            pl.BlockSpec(memory_space=pl.ANY),
            pl.BlockSpec(memory_space=pl.ANY),
        ],
        out_specs=pl.BlockSpec(memory_space=pltpu.VMEM),
        scratch_shapes=[
            pltpu.VMEM((4 * OWN, D), bf16),
            pltpu.VMEM((HALF, D), bf16),
            pltpu.VMEM((3, D, WIDTH), bf16),
            pltpu.VMEM((4, WIDTH, D), bf16),
            pltpu.VMEM((3, 1024, WIDTH), bf16),
            pltpu.VMEM((4 * OWN, WIDTH), bf16),
            pltpu.VMEM((1024, WIDTH), bf16),
            pltpu.VMEM((256, 4 * WIDTH), bf16),
            pltpu.VMEM((256, D), bf16),
            pltpu.VMEM((256, D), bf16),
            pltpu.VMEM((OWN, 4 * WIDTH), bf16),
            dma((5,)), dma(()), dma((3,)), dma((3,)), dma((3,)), dma((3,)),
            dma(()), dma(()), dma(()), dma(()), dma((2,)), dma((2,)),
            dma((2,)), dma((2,)), dma((2,)), dma((2,)), dma(()), dma(()),
            dma(()), dma(()), dma((2,)), dma((2,)), dma(()), dma(()),
        ],
        compiler_params=pltpu.CompilerParams(
            collective_id=0, has_side_effects=True, vmem_limit_bytes=64000 * 1024
        ),
    )(hidden_in, norm_gain.reshape(1, D), w_qkv, w_out)


def solution(mesh):
    return jax.shard_map(
        on_device,
        mesh=mesh,
        in_specs=(P(("seq", "tp"), None), P(), P(None, None, "tp"), P("tp", None)),
        out_specs=P(("seq", "tp"), None),
        check_vma=False,
    )
```
